256 devices in a mesh: gx: 16 (over y, x), gy: 8 (over z), gz: 2 (over core).
Axes of the slice: x: 4, y: 4, z: 8, core: 2. Of those that a mesh axis runs over, the one named last changes fastest.
Arguments:
- tokens_in: bfloat16 [2048, 12288], P('gx', ('gz', 'gy')), may hold values from -20.4 to 20.4
- qkv_weight: bfloat16 [96, 128, 64, 384], P('gz', 'gx', 'gy'), may hold values from -0.0546875 to 0.0546875
- qkv_mask: int32 [96, 64, 3], P('gz', 'gy'), may hold values from 0 to 1, as said below
- out_weight: bfloat16 [64, 128, 12288], P('gy', 'gx', 'gz'), may hold values from -0.0625 to 0.0625
- out_mask: int32 [64, 96], P('gy', 'gz'), may hold values from 0 to 1, as said below
Outputs:
- mixed: bfloat16 [2048, 12288], P(('gx', 'gy'), 'gz')
The draws below stay inside these ranges and needn't reach their ends.
Inputs may be any that keep to these rules, and one draw needn't show every extreme that they name: `qkv_mask`: exactly half of the blocks are kept within each face of 48 row blocks by 8 heads by 3 (row blocks r * 48 to r * 48 + 47, heads g * 8 to g * 8 + 7). `out_mask`: exactly half of the blocks are kept within each face of 8 heads by 48 column blocks, aligned as for qkv_mask.
All inputs are finite; a program needn't handle non-finite values.
Results may differ from the reference program's by a relative error of at most 0.005.
The reference program's roundings to bfloat16 on the way count: a program that leaves them out, or rounds other values in their place, can miss the bound.
Values may be sent and summed in bfloat16 or wider, within the bound.
No kernel may reach another device: no remote copies, remote signals or barrier semaphores. Data moves between devices by JAX's collectives and lax.ppermute only.
A program may use at most 192 MiB of HBM per device.

```python
import math
import jax
import jax.numpy as jnp
from jax import lax

D = 12288
HEADS = 64
HEAD = 128
TOKENS = 2048
BLOCK = 128
DB = 96
RB = 48
HG = 8


def draw_tokens_in(key, part):
    normal_base = jnp.clip(jax.random.normal(key, (TOKENS, D), jnp.float32), -4.0, 4.0)
    return normal_base.astype(jnp.bfloat16)


def face_masks(key, outer, inner, face_shape):
    face_count = math.prod(face_shape)

    def face_draw(number):
        shuffled = jax.random.permutation(jax.random.fold_in(key, number), face_count)
        return (shuffled < face_count // 2).astype(jnp.int32).reshape(face_shape)
    grid_draws = jax.vmap(face_draw)(jnp.arange(outer * inner))
    return grid_draws.reshape((outer, inner) + tuple(face_shape))


def draw_qkv_mask(key, part):
    face_grid = face_masks(jax.random.fold_in(key, 21), DB // RB, HEADS // HG, (RB, HG, 3))
    return jnp.transpose(face_grid, (0, 2, 1, 3, 4)).reshape(DB, HEADS, 3)


def draw_out_mask(key, part):
    face_grid = face_masks(jax.random.fold_in(key, 22), HEADS // HG, DB // RB, (HG, RB))
    return jnp.transpose(face_grid, (0, 2, 1, 3)).reshape(HEADS, DB)


def levels(own_key, extent, cuts, smallest, high):
    gain, own = 1.0, jax.random.fold_in(own_key, 6)
    for dim, shards_of in cuts:
        heights = jnp.exp(jax.random.uniform(jax.random.fold_in(own, dim), (shards_of,), jnp.float32, smallest / len(cuts), high / len(cuts)))
        gain = gain * jnp.repeat(heights, extent[dim] // shards_of).reshape([-1 if axis == dim else 1 for axis in range(len(extent))])
    return gain


def centred(key, extent, width, most, cuts=(), kind=jnp.bfloat16):
    factor_of = levels(key, extent, cuts, -0.22, 0.18) if cuts else 1.0
    result = jax.random.normal(key, extent, jnp.float32) * width * factor_of
    return jnp.minimum(jnp.maximum(result, -most), most).astype(kind)


def setup_inputs(seed: int = 0) -> dict:
    splits = jax.random.split(jax.random.key(seed), 6)
    return {
        "tokens_in": draw_tokens_in(jax.random.fold_in(splits[5], 71), 0),
        "qkv_weight": centred(splits[1], (DB, BLOCK, HEADS, 3 * HEAD), D ** -0.5, 0.0546875, ((0, 2), (1, 16), (2, 8))),
        "qkv_mask": draw_qkv_mask(jax.random.fold_in(splits[5], 71), 0),
        "out_weight": centred(splits[3], (HEADS, HEAD, D), (HEADS * HEAD) ** -0.5, 0.0625, ((0, 8), (1, 16), (2, 2))),
        "out_mask": draw_out_mask(jax.random.fold_in(splits[5], 71), 0),
    }


def attend_head(packed):
    queries, keys_all, values_all = packed
    scores = jnp.dot(queries, keys_all.T, preferred_element_type=jnp.float32) * (HEAD ** -0.5)
    positions = jnp.arange(TOKENS)
    allowed = positions[None, :] <= positions[:, None]
    scores = jnp.where(allowed, scores, -1e30)
    row_top = jnp.max(scores, axis=1, keepdims=True)
    weights = jnp.exp(scores - row_top)
    normed = (weights / jnp.sum(weights, axis=1, keepdims=True)).astype(jnp.bfloat16)
    return jnp.dot(normed, values_all, preferred_element_type=jnp.float32).astype(jnp.bfloat16)


def reference(tokens_in, qkv_weight, qkv_mask, out_weight, out_mask):
    keep_qkv = qkv_mask.astype(jnp.bfloat16)[:, None, :, :, None]
    shaped = qkv_weight.reshape(DB, BLOCK, HEADS, 3, HEAD) * keep_qkv
    projected = jnp.dot(tokens_in, shaped.reshape(D, HEADS * 3 * HEAD), preferred_element_type=jnp.float32).astype(jnp.bfloat16)
    by_head = jnp.transpose(projected.reshape(TOKENS, HEADS, 3, HEAD), (1, 2, 0, 3))
    attended = lax.map(attend_head, (by_head[:, 0], by_head[:, 1], by_head[:, 2]))
    mixed_in = jnp.transpose(attended, (1, 0, 2)).reshape(TOKENS, HEADS * HEAD)
    keep_out = out_mask.astype(jnp.bfloat16)[:, None, :, None]
    out_shaped = out_weight.reshape(HEADS, HEAD, DB, BLOCK) * keep_out
    return jnp.dot(mixed_in, out_shaped.reshape(HEADS * HEAD, D), preferred_element_type=jnp.float32).astype(jnp.bfloat16)
```

```python
import jax
import jax.numpy as jnp
from jax import lax
from jax.experimental import pallas as pl
from jax.experimental.pallas import tpu as pltpu
from jax.sharding import Mesh, PartitionSpec as P

HEAD = 128
BLOCK = 128
SIDE = 4
bf16 = jnp.bfloat16
f32 = jnp.float32


PAIRS = {
    "bx": ("x", (1, 0, 3, 2)),
    "ax": ("x", (3, 2, 1, 0)),
    "by": ("y", (1, 0, 3, 2)),
    "ay": ("y", (3, 2, 1, 0)),
}
DIMS = ("bx", "by", "ax", "ay")
ORDERS = tuple(DIMS[k:] + DIMS[:k] for k in range(4))


def swap(value, dim):
    axis, partner = PAIRS[dim]
    return lax.ppermute(value, axis, [(i, partner[i]) for i in range(SIDE)])


def shift(value, step):
    return lax.ppermute(value, "gy", [(i, (i + step) % 8) for i in range(8)])


def other_core(value):
    return lax.ppermute(value, "gz", [(0, 1), (1, 0)])


def pick(array, index, axis=0):
    return lax.dynamic_index_in_dim(array, index, axis, keepdims=False)


def bits(place):
    high = place // 2
    return high, high ^ (place % 2)


def place_of(high, low):
    return high * 2 + (high ^ low)


def project_kernel(pieces, where_ref, *refs):
    mine, theirs = refs[:pieces], refs[pieces : 2 * pieces]
    w_mine, w_theirs = refs[2 * pieces], refs[2 * pieces + 1]
    outs = refs[2 * pieces + 2 : 2 * pieces + 10]
    x_scr, w_scr = refs[2 * pieces + 10 :]
    step = pl.program_id(0)

    @pl.when(step == 0)
    def _():
        half = w_mine.shape[1]
        for h in range(SIDE):
            w_scr[h, :half] = w_mine[h]
            w_scr[h, half:] = w_theirs[h]
        for block in range(16):
            column = jnp.concatenate([r[block] for r in mine + theirs], axis=0)
            x_scr[block] = column.T

    for colour in range(4):
        for side in range(2):
            number = side * 8 + step
            flip = {}
            for position, dim in enumerate(ORDERS[colour]):
                flip[dim] = (number // (8 >> position)) % 2
            ax, bx = where_ref[0] ^ flip["ax"], where_ref[1] ^ flip["bx"]
            ay, by = where_ref[2] ^ flip["ay"], where_ref[3] ^ flip["by"]
            block = place_of(ax, bx) + 4 * colour
            head = place_of(ay, by)
            outs[colour * 2 + side][0] = jnp.dot(
                x_scr[block], w_scr[head], preferred_element_type=f32
            )


def project(where, mine, theirs, w_mine, w_theirs):
    pieces = len(mine)
    blocks, feats, tok = mine[0].shape
    heads, half, triple = w_mine.shape
    whole = lambda a: pl.BlockSpec(a.shape, lambda i, s: (0,) * a.ndim)
    operands = list(mine) + list(theirs) + [w_mine, w_theirs]
    flops = 2 * blocks * tok * 2 * half * heads * triple
    return pl.pallas_call(
        lambda *refs: project_kernel(pieces, *refs),
        grid_spec=pltpu.PrefetchScalarGridSpec(
            num_scalar_prefetch=1,
            grid=(8,),
            in_specs=[whole(a) for a in operands],
            out_specs=[pl.BlockSpec((1, tok, triple), lambda i, s: (i, 0, 0))] * 8,
            scratch_shapes=[
                pltpu.VMEM((blocks, tok, 2 * half), bf16),
                pltpu.VMEM((heads, 2 * half, triple), bf16),
            ],
        ),
        out_shape=[jax.ShapeDtypeStruct((8, tok, triple), f32)] * 8,
        cost_estimate=pl.CostEstimate(
            flops=flops, bytes_accessed=20_000_000, transcendentals=0
        ),
    )(where, *operands)


def body(tokens_in, qkv_weight, qkv_mask, out_weight, out_mask):
    my_y, my_x = lax.axis_index("y"), lax.axis_index("x")
    my_z, my_c = lax.axis_index("gy"), lax.axis_index("gz")
    tok_rows = tokens_in.shape[0]
    row_blocks, sub_rows, group_heads, triple = qkv_weight.shape
    own_heads = group_heads // 2

    out_full = lax.all_gather(out_weight, ("y", "x"), axis=1, tiled=True)

    own_rb = tokens_in.shape[1] // BLOCK
    feats = own_rb * sub_rows
    xt = tokens_in.T.reshape(own_rb, SIDE * SIDE, sub_rows, tok_rows).transpose(1, 0, 2, 3)
    xt = lax.all_to_all(
        xt.reshape(SIDE * SIDE, feats, tok_rows), ("y", "x"), 0, 0, tiled=True
    )
    ups, downs = [], []
    up, down = xt, xt
    for step in (1, 2, 3):
        up, down = shift(up, 1), shift(down, -1)
        ups.append(up)
        downs.append(down)
    far_a = shift(up[:8], 1)
    far_b = shift(down[8:], -1)
    far = jnp.concatenate([far_a, far_b], axis=0)
    mine = [xt, downs[0], downs[1], downs[2], far, ups[2], ups[1], ups[0]]
    near = other_core(jnp.stack([mine[i] for i in (0, 1, 2, 6, 7)]))
    rest = other_core(jnp.stack([mine[i] for i in (3, 4, 5)]))
    theirs = [near[0], near[1], near[2], rest[0], rest[1], rest[2], near[3], near[4]]

    keep = qkv_mask.astype(bf16)[:, None, :, :, None]
    masked = qkv_weight.reshape(row_blocks, sub_rows, group_heads, 3, HEAD) * keep
    masked = masked.reshape(8, feats, group_heads, triple)
    masked = jnp.roll(masked, -my_z, axis=0)
    masked = masked.transpose(2, 0, 1, 3).reshape(2, own_heads, 8 * feats, triple)
    w_mine = pick(masked, my_c)
    w_theirs = other_core(pick(masked, 1 - my_c))

    ax, bx = bits(my_x)
    ay, by = bits(my_y)
    where = jnp.stack([ax, bx, ay, by]).astype(jnp.int32)
    outs = project(where, mine, theirs, w_mine, w_theirs)
    keeps, sends = list(outs[0::2]), list(outs[1::2])
    for step in range(4):
        got = [swap(sends[k], ORDERS[k][step]) for k in range(4)]
        for k in range(4):
            total = keeps[k] + got[k]
            half = total.shape[0] // 2
            if half:
                keeps[k], sends[k] = total[:half], total[half:]
            else:
                keeps[k] = total
    own = jnp.concatenate(keeps, axis=0).astype(bf16)

    queries = own[:, :, :HEAD].reshape(4 * tok_rows, HEAD)
    kv = own[:, :, HEAD:]
    kv_a, kv_b = kv[:2], kv[2:]
    a1, b1 = swap(kv_a, "bx"), swap(kv_b, "ax")
    a_two, b_two = jnp.stack([kv_a, a1]), jnp.stack([kv_b, b1])
    a2, b2 = swap(a_two, "ax"), swap(b_two, "bx")
    kv_all = jnp.concatenate([a_two, a2, b_two, b2], axis=0).reshape(16 * tok_rows, 2 * HEAD)
    in_block = jnp.arange(tok_rows)
    places = [place_of(ax ^ i, bx ^ j) for i, j in ((0, 0), (0, 1), (1, 0), (1, 1))]
    key_pos = [(places[n] + 4 * j) * tok_rows + in_block for n in range(4) for j in (0, 1)]
    key_pos += [
        (places[n] + 4 * j) * tok_rows + in_block for n in (0, 2, 1, 3) for j in (2, 3)
    ]
    key_pos = jnp.concatenate(key_pos)
    query_pos = jnp.concatenate([(my_x + 4 * j) * tok_rows + in_block for j in range(4)])
    scores = lax.dot_general(
        queries, kv_all[:, :HEAD], (((1,), (1,)), ((), ())), preferred_element_type=f32
    ) * HEAD ** (-0.5)
    scores = jnp.where(key_pos[None, :] <= query_pos[:, None], scores, -1e30)
    row_top = jnp.max(scores, axis=1, keepdims=True)
    weights = jnp.exp(scores - row_top)
    normed = (weights / jnp.sum(weights, axis=1, keepdims=True)).astype(bf16)
    attended = jnp.dot(normed, kv_all[:, HEAD:], preferred_element_type=f32).astype(bf16)

    att = lax.all_to_all(attended.reshape(SIDE, tok_rows, HEAD), "y", 0, 0, tiled=True)
    att_other = other_core(att)
    low = jnp.where(my_c == 0, att, att_other)
    high = jnp.where(my_c == 0, att_other, att)
    flat_in = jnp.concatenate([low, high], axis=0).transpose(1, 0, 2)
    flat_in = flat_in.reshape(tok_rows, group_heads * HEAD)
    out_heads, _, out_cols = out_weight.shape
    keep_out = out_mask.astype(bf16)[:, None, :, None]
    out_masked = out_full.reshape(out_heads, HEAD, out_cols // BLOCK, BLOCK) * keep_out
    summed = jnp.dot(
        flat_in, out_masked.reshape(out_heads * HEAD, out_cols), preferred_element_type=f32
    ).astype(bf16)

    rows = tok_rows // 8
    half = out_cols // 2

    def block(offset):
        return lax.dynamic_slice_in_dim(summed, ((my_z + offset) % 8) * rows, rows, axis=0)

    def add(left, right):
        return (left.astype(f32) + right.astype(f32)).astype(bf16)

    far = block(4)
    up, down = shift(far[:, :half], 1), shift(far[:, half:], -1)
    own_up, own_down = block(3), block(-3)
    up = jnp.concatenate([add(own_up[:, :half], up), own_up[:, half:]], axis=1)
    down = jnp.concatenate([own_down[:, :half], add(own_down[:, half:], down)], axis=1)
    up, down = shift(up, 1), shift(down, -1)
    for distance in (2, 1):
        up, down = add(block(distance), up), add(block(-distance), down)
        up, down = shift(up, 1), shift(down, -1)
    return (block(0).astype(f32) + up.astype(f32) + down.astype(f32)).astype(bf16)


def solution(mesh):
    plane = Mesh(mesh.devices.reshape(SIDE, SIDE, 8, 2), ("y", "x", "gy", "gz"))
    return jax.shard_map(
        body,
        mesh=plane,
        in_specs=(
            P(("y", "x"), ("gz", "gy")),
            P("gz", ("y", "x"), "gy", None),
            P("gz", "gy", None),
            P("gy", ("y", "x"), "gz"),
            P("gy", "gz"),
        ),
        out_specs=P(("y", "x", "gy"), "gz"),
        check_vma=False,
    )
```

```python
import functools

import jax
import jax.numpy as jnp
from jax import lax
from jax.experimental import pallas as pl
from jax.experimental.pallas import tpu as pltpu
from jax.sharding import Mesh, PartitionSpec as P

HEAD = 128
BLOCK = 128
SIDE = 4
bf16 = jnp.bfloat16
f32 = jnp.float32


PAIRS = {
    "bx": ("x", (1, 0, 3, 2)),
    "ax": ("x", (3, 2, 1, 0)),
    "by": ("y", (1, 0, 3, 2)),
    "ay": ("y", (3, 2, 1, 0)),
}
DIMS = ("bx", "by", "ax", "ay")
ORDERS = tuple(DIMS[k:] + DIMS[:k] for k in range(4))


def swap(value, dim):
    axis, partner = PAIRS[dim]
    return lax.ppermute(value, axis, [(i, partner[i]) for i in range(SIDE)])


def shift(value, step):
    return lax.ppermute(value, "gy", [(i, (i + step) % 8) for i in range(8)])


def other_core(value):
    return lax.ppermute(value, "gz", [(0, 1), (1, 0)])


def pick(array, index, axis=0):
    return lax.dynamic_index_in_dim(array, index, axis, keepdims=False)


def bits(place):
    high = place // 2
    return high, high ^ (place % 2)


def place_of(high, low):
    return high * 2 + (high ^ low)


def project_kernel(colour, where_ref, *refs):
    pieces, (w_ref, keep_ref, send_ref, x_scr) = refs[:-4], refs[-4:]
    tok = keep_ref.shape[1]
    flips = ((0, 0), (0, 1), (1, 0), (1, 1))
    for n, (high, low) in enumerate(flips):
        block = place_of(where_ref[0] ^ high, where_ref[1] ^ low) + 4 * colour
        parts = []
        for ref in pieces:
            at = block - ref.shape[0] * (colour // 2) if ref.shape[0] == 8 else block
            parts.append(ref[at])
        x_scr[n * tok : (n + 1) * tok] = jnp.concatenate(parts, axis=0).T
    for high, low in flips:
        head = place_of(where_ref[2] ^ high, where_ref[3] ^ low)
        result = jnp.dot(x_scr[...], w_ref[head], preferred_element_type=f32)
        for n, (x_high, x_low) in enumerate(flips):
            flip = {"ax": x_high, "bx": x_low, "ay": high, "by": low}
            number = 0
            for dim in ORDERS[colour]:
                number = number * 2 + flip[dim]
            target = send_ref if number >= 8 else keep_ref
            target[number % 8] = result[n * tok : (n + 1) * tok]


def project(colour, where, pieces, weight):
    tok, (heads, depth, triple) = HEAD, weight.shape
    vmem = pl.BlockSpec(memory_space=pltpu.VMEM)
    return pl.pallas_call(
        functools.partial(project_kernel, colour),
        in_specs=[pl.BlockSpec(memory_space=pltpu.SMEM)] + [vmem] * (len(pieces) + 1),
        out_specs=[vmem, vmem],
        scratch_shapes=[pltpu.VMEM((SIDE * tok, depth), bf16)],
        out_shape=[jax.ShapeDtypeStruct((8, tok, triple), f32)] * 2,
        cost_estimate=pl.CostEstimate(
            flops=2 * SIDE * tok * depth * heads * triple,
            bytes_accessed=6_000_000,
            transcendentals=0,
        ),
    )(where, *pieces, weight)


def body(tokens_in, qkv_weight, qkv_mask, out_weight, out_mask):
    my_y, my_x = lax.axis_index("y"), lax.axis_index("x")
    my_z, my_c = lax.axis_index("gy"), lax.axis_index("gz")
    tok_rows = tokens_in.shape[0]
    row_blocks, sub_rows, group_heads, triple = qkv_weight.shape
    own_heads = group_heads // 2

    ax, bx = bits(my_x)
    ay, by = bits(my_y)
    where = jnp.stack([ax, bx, ay, by]).astype(jnp.int32)
    flips = ((0, 0), (0, 1), (1, 0), (1, 1))

    own_rb = tokens_in.shape[1] // BLOCK
    feats = own_rb * sub_rows
    xt = tokens_in.T.reshape(own_rb, SIDE * SIDE, sub_rows, tok_rows).transpose(1, 0, 2, 3)
    xt = lax.all_to_all(
        xt.reshape(SIDE * SIDE, feats, tok_rows), ("y", "x"), 0, 0, tiled=True
    )
    ups, downs = [], []
    up, down = xt, xt
    for step in (1, 2, 3):
        up, down = shift(up, 1), shift(down, -1)
        ups.append(up)
        downs.append(down)
    far_a = shift(up[:8], 1)
    far_b = shift(down[8:], -1)
    mine = [xt, downs[0], downs[1], downs[2], far_a, far_b, ups[2], ups[1], ups[0]]
    theirs = [other_core(piece) for piece in mine]

    out_heads, out_sub, out_cols = out_weight.shape
    col = out_cols // SIDE
    wo = out_weight.reshape(out_heads, out_sub, SIDE, col).transpose(2, 0, 1, 3)
    wo = lax.all_to_all(wo, "y", 0, 0, tiled=True)
    wo_a, wo_b = wo[:2], wo[2:]
    a1, b1 = swap(wo_a, "bx"), swap(wo_b, "ax")
    a_two, b_two = jnp.stack([wo_a, a1]), jnp.stack([wo_b, b1])
    a2, b2 = swap(a_two, "ax"), swap(b_two, "bx")
    wo_a = jnp.concatenate([a_two, a2], axis=0)
    wo_b = jnp.concatenate([b_two, b2], axis=0)
    by_x = []
    for place in range(SIDE):
        high, low = bits(place)
        dh, dl = high ^ ax, low ^ bx
        by_x.append(jnp.concatenate([pick(wo_a, dh * 2 + dl), pick(wo_b, dl * 2 + dh)], axis=0))
    wo = jnp.stack(by_x, axis=1)
    wo = wo.transpose(2, 0, 1, 3, 4).reshape(out_heads, HEAD, col // BLOCK, BLOCK)
    keep_out = lax.dynamic_slice_in_dim(out_mask, my_y * (col // BLOCK), col // BLOCK, axis=1)
    wo = (wo * keep_out.astype(bf16)[:, None, :, None]).reshape(out_heads * HEAD, col)

    keep = qkv_mask.astype(bf16)[:, None, :, :, None]
    masked = qkv_weight.reshape(row_blocks, sub_rows, group_heads, 3, HEAD) * keep
    masked = masked.reshape(8, feats, group_heads, triple)
    masked = jnp.roll(masked, -my_z, axis=0)
    masked = masked.transpose(2, 0, 1, 3).reshape(2, own_heads, 8 * feats, triple)
    w_mine = pick(masked, my_c)
    w_theirs = other_core(pick(masked, 1 - my_c))

    weight = jnp.concatenate([w_mine, w_theirs], axis=1)
    keeps, sends = [], []
    for k in range(4):
        unused = 5 if k < 2 else 4
        pieces = [p for i, p in enumerate(mine + theirs) if i % 9 != unused]
        kept, sent = project(k, where, pieces, weight)
        keeps.append(kept)
        sends.append(sent)
    for step in range(4):
        for k in range(4):
            got = swap(sends[k], ORDERS[k][step])
            half = got.shape[0] // 2
            if half:
                sends[k] = keeps[k][half:] + got[half:]
                keeps[k] = keeps[k][:half] + got[:half]
            else:
                keeps[k] = keeps[k] + got
    own = jnp.concatenate(keeps, axis=0).astype(bf16)

    queries = own[:, :, :HEAD].reshape(4 * tok_rows, HEAD)
    kv = own[:, :, HEAD:]
    kv_all = lax.all_to_all(
        jnp.broadcast_to(kv[None], (SIDE,) + kv.shape), "x", 0, 0, tiled=True
    ).reshape(16 * tok_rows, 2 * HEAD)
    in_block = jnp.arange(tok_rows)
    key_pos = jnp.concatenate(
        [(x + 4 * j) * tok_rows + in_block for x in range(SIDE) for j in range(4)]
    )
    query_pos = jnp.concatenate([(my_x + 4 * j) * tok_rows + in_block for j in range(4)])
    scores = lax.dot_general(
        queries, kv_all[:, :HEAD], (((1,), (1,)), ((), ())), preferred_element_type=f32
    ) * HEAD ** (-0.5)
    scores = jnp.where(key_pos[None, :] <= query_pos[:, None], scores, -1e30)
    row_top = jnp.max(scores, axis=1, keepdims=True)
    weights = jnp.exp(scores - row_top)
    normed = (weights / jnp.sum(weights, axis=1, keepdims=True)).astype(bf16)
    attended = jnp.dot(normed, kv_all[:, HEAD:], preferred_element_type=f32).astype(bf16)

    att = lax.all_to_all(
        jnp.broadcast_to(attended[None], (SIDE,) + attended.shape), "y", 0, 0, tiled=True
    )
    att_other = other_core(att)
    low = jnp.where(my_c == 0, att, att_other)
    high = jnp.where(my_c == 0, att_other, att)
    flat_in = jnp.concatenate([low, high], axis=0).transpose(1, 0, 2)
    flat_in = flat_in.reshape(4 * tok_rows, group_heads * HEAD)
    summed = jnp.dot(flat_in, wo, preferred_element_type=f32).astype(bf16)

    rows = tok_rows // 8
    summed = summed.reshape(SIDE, 8, rows, col)

    def block(offset):
        return pick(summed, (my_z + offset) % 8, 1)

    def add(left, right):
        return (left.astype(f32) + right.astype(f32)).astype(bf16)

    far = block(4)
    up, down = shift(far[:2], 1), shift(far[2:], -1)
    own_up, own_down = block(3), block(-3)
    up = jnp.concatenate([add(own_up[:2], up), own_up[2:]], axis=0)
    down = jnp.concatenate([own_down[:2], add(own_down[2:], down)], axis=0)
    up, down = shift(up, 1), shift(down, -1)
    for distance in (2, 1):
        up, down = add(block(distance), up), add(block(-distance), down)
        up, down = shift(up, 1), shift(down, -1)
    final = (block(0).astype(f32) + up.astype(f32) + down.astype(f32)).astype(bf16)
    got = lax.all_to_all(final, "y", 0, 0, tiled=True)
    return got.transpose(1, 0, 2).reshape(rows, out_cols)


def solution(mesh):
    plane = Mesh(mesh.devices.reshape(SIDE, SIDE, 8, 2), ("y", "x", "gy", "gz"))
    return jax.shard_map(
        body,
        mesh=plane,
        in_specs=(
            P(("y", "x"), ("gz", "gy")),
            P("gz", ("y", "x"), "gy", None),
            P("gz", "gy", None),
            P("gy", ("y", "x"), "gz"),
            P("gy", "gz"),
        ),
        out_specs=P(("y", "x", "gy"), "gz"),
        check_vma=False,
    )
```
